32 devices in a mesh: slab: 8 (over y, x, core), term: 4 (over z).
Axes of the slice: x: 2, y: 2, z: 4, core: 2. Of those that a mesh axis runs over, the one named last changes fastest.
Arguments:
- panels: float32 [64, 1024], P(None, 'term'), may hold values from -0.1875 to 0.1875
- block_phase: int32 [2, 64], P(None, 'term'), may hold values from 0 to 4194303
- target_owner: int32 [16384, 1], P(('slab', 'term')), may hold values from 0 to 31; in each aligned block of 512 rows (0 to 511, 512 to 1023, ...) at most 32 rows name the same one
- target_cell: int32 [16384], P(('slab', 'term')), may hold values from 0 to 6143
- target_offset: int32 [16384], P(('slab', 'term')), may hold values from 0 to 255
Outputs:
- grid_values: float32 [64, 196608], P(None, ('slab', 'term'))
- target_values: float32 [64, 16384], P(None, ('slab', 'term'))
The draws below stay inside these ranges and needn't reach their ends.
Inputs may be any that keep to these rules, and one draw needn't show every extreme that they name: `target_owner`: among the 512 targets of one device no owner appears more than 32 times, and some owner appears exactly 32 times.
All inputs are finite; a program needn't handle non-finite values.
Results may differ from the reference program's by a relative error of at most 0.0003.
Values sent between devices are 32-bit elements; how exact they have to be, the bound alone decides.
A program may use at most 256 MiB of HBM per device.

```python
import math
import jax
import jax.numpy as jnp
import numpy as np
from jax import lax

CH = 32
ORDER = 16
TAPS = 256
OFFQ = 256
ROOTQ = 2048
GS = 6144
TGT_DEV = 512
PHASEQ = 4194304
BLOCKS = 64
NGRID = 196608
TARGETS = 16384
CAP = 32
DEVICES = 32


def place_ends(entries, rng, low, largest):
    dims = entries.shape
    index_at = [jax.random.randint(jax.random.fold_in(rng, axis), (), 0, dims[axis]) for axis in range(len(dims))]
    entries = entries.at[tuple(index_at)].set(low)
    longest = dims.index(max(dims))
    index_at[longest] = (index_at[longest] + 1) % dims[longest]
    return entries.at[tuple(index_at)].set(largest)


def shard_levels(stream_key, shape, pieces, low, largest):
    def one(axis_at, parts):
        heights = jax.random.uniform(jax.random.fold_in(jax.random.fold_in(stream_key, 6), axis_at), (parts,), jnp.float32, low / len(pieces), largest / len(pieces))
        return jnp.repeat(jnp.exp(heights), shape[axis_at] // parts).reshape((-1,) + (1,) * (len(shape) - axis_at - 1))

    gain = one(*pieces[0])
    for cut in pieces[1:]:
        gain = gain * one(*cut)
    return gain


def assign_block(own_key, own, number, rows, count, top, reach, lean):
    ranking = jax.random.permutation(own_key, count)
    crowded, ordinary = portions_of(count, rows * top, reach, lean, True), portions_of(count, rows * top, reach, lean, False)
    places = jnp.arange(count)

    def named(sizes, offset_by):
        used = int((sizes > 0).sum())
        fixed = max(1, used // 4)
        passed = fixed + (places - fixed + offset_by * (used - fixed)) % max(1, count - fixed)
        return jnp.zeros((count,), jnp.int32).at[ranking[jnp.where(places < fixed, places, passed)]].set(jnp.asarray(sizes, jnp.int32))

    sizes = jnp.where(number % 4 == 0, named(crowded, number // 4), named(ordinary, number - number // 4 - 1))
    mixed = jax.random.permutation(jax.random.fold_in(own, 3), count)
    giver, sink = mixed[0:count // 2 * 2:2], mixed[1:count // 2 * 2:2]
    slack = jnp.minimum(sizes[giver] - 1, reach - sizes[sink]) // 2
    slack = jnp.where((giver == ranking[0]) | (sink == ranking[0]) | (sizes[sink] == 0), 0, jnp.maximum(slack, 0))
    passed = jax.random.randint(jax.random.fold_in(own, 4), (count // 2,), 0, 1 << 20) % (slack + 1)
    sizes = sizes.at[giver].add(-passed).at[sink].add(passed)
    items = jnp.searchsorted(jnp.cumsum(sizes), jnp.arange(rows * top), side="right").astype(jnp.int32)
    listing = items.reshape(top, rows).T
    listing = listing[jax.random.permutation(jax.random.fold_in(own, 1), rows)]
    offset_by = jax.random.randint(jax.random.fold_in(own, 2), (rows, 1), 0, top)
    return jnp.take_along_axis(listing, (jnp.arange(top)[None, :] + offset_by) % top, axis=1)


def portions_of(amount, total, reach, slope, full):
    portions = [(1 << 20) // math.isqrt(rank ** slope) + 1 for rank in range(1, amount + 1)]
    largest = reach if full else min(reach, max(-(-total // amount), total * portions[0] // sum(portions)))
    least = 1 if total - largest >= amount - 1 else 0
    counts, spare = [largest] + [least] * (amount - 1), total - largest - least * (amount - 1)
    while spare > 0:
        free = [i for i in range(1, amount) if counts[i] < largest] or [i for i in range(1, amount) if counts[i] < reach]
        pool, remaining = sum([portions[i] for i in free]), spare
        for i in free:
            addition = min(reach - counts[i], max(1, remaining * portions[i] // pool), spare)
            counts[i] = counts[i] + addition
            spare = spare - addition
    return np.array(counts)


def noise(key, shape, scale, reach, pieces=(), kind=jnp.bfloat16):
    drawn = scale * jax.random.normal(key, shape, jnp.float32)
    if pieces:
        drawn = drawn * shard_levels(key, shape, pieces, -0.22, 0.18)
    return jnp.clip(drawn, -reach, reach).astype(kind)


def setup_inputs(seed: int = 0) -> dict:
    keys = jax.random.split(jax.random.key(seed), 6)
    panels = noise(keys[0], (2 * CH, BLOCKS * ORDER), (BLOCKS * ORDER) ** -0.5, 0.1875, ((1, 4),), jnp.float32)
    block_phase = place_ends(jax.random.randint(keys[1], (2, BLOCKS), 0, PHASEQ), jax.random.fold_in(keys[1], 1), 0, PHASEQ - 1).astype(jnp.int32)
    target_owner_keys = jax.random.split(jax.random.fold_in(keys[2], 1), TARGETS // TGT_DEV)
    target_owner_turns = jax.random.permutation(jax.random.fold_in(keys[2], 3), TARGETS // TGT_DEV)
    target_owner = jax.vmap(lambda own, number: assign_block(jax.random.fold_in(keys[2], 2), own, number, TGT_DEV, DEVICES, 1, CAP, 2))(target_owner_keys, target_owner_turns).reshape((TARGETS, 1))
    target_cell = place_ends(jax.random.randint(keys[3], (TARGETS,), 0, GS), jax.random.fold_in(keys[3], 1), 0, GS - 1).astype(jnp.int32)
    target_offset = place_ends(jax.random.randint(keys[4], (TARGETS,), 0, OFFQ), jax.random.fold_in(keys[4], 1), 0, OFFQ - 1).astype(jnp.int32)
    return dict(panels=panels, block_phase=block_phase, target_owner=target_owner, target_cell=target_cell, target_offset=target_offset)


def chebyshev(xpos, order):
    rows = [jnp.ones_like(xpos), xpos]
    for j in range(2, order):
        rows.append(2.0 * xpos * rows[-1] - rows[-2])
    return jnp.stack(rows[:order], 0)


def block_turns(phases, gpos):
    wrapped = gpos % PHASEQ
    g_high = wrapped // ROOTQ
    g_low = wrapped % ROOTQ
    p_high = phases[1] // ROOTQ
    p_low = phases[1] % ROOTQ
    cross = (g_high[None, :] * p_low[:, None] + g_low[None, :] * p_high[:, None]) % ROOTQ
    total = phases[0][:, None] + cross * ROOTQ + g_low[None, :] * p_low[:, None]
    return (total % PHASEQ).astype(jnp.int32)


def grid_terms(coeffs, phases, gpos):
    nblk = phases.shape[1]
    order = coeffs.shape[1] // nblk
    half = coeffs.shape[0] // 2
    width = gpos.shape[0]
    local = gpos - (gpos // GS) * GS
    xpos = (2 * local + 1).astype(jnp.float32) / GS - 1.0
    cheb = chebyshev(xpos, order)
    turns = block_turns(phases, gpos)
    angle = turns.astype(jnp.float32) * (2.0 * math.pi / PHASEQ)
    basis_cos = (jnp.cos(angle)[:, None, :] * cheb[None, :, :]).reshape(nblk * order, width)
    basis_sin = (jnp.sin(angle)[:, None, :] * cheb[None, :, :]).reshape(nblk * order, width)
    with_cos = jnp.dot(coeffs, basis_cos, precision=lax.Precision.HIGHEST, preferred_element_type=jnp.float32)
    with_sin = jnp.dot(coeffs, basis_sin, precision=lax.Precision.HIGHEST, preferred_element_type=jnp.float32)
    real_part = with_cos[:half] - with_sin[half:]
    imag_part = with_sin[:half] + with_cos[half:]
    return jnp.concatenate([real_part, imag_part], 0)


def kernel_rows(offsets):
    frac = (offsets.astype(jnp.float32) + 0.5) / OFFQ
    place = jnp.arange(TAPS, dtype=jnp.int32)
    dist = (place - TAPS // 2 + 1).astype(jnp.float32)[None, :] - frac[:, None]
    parity = jnp.where(place % 2 == 0, 1.0, -1.0).astype(jnp.float32)
    return parity[None, :] * jnp.sin(math.pi * frac)[:, None] / (math.pi * dist) * jnp.exp(-18.0 * dist * dist / (TAPS * TAPS))


def reference(panels, block_phase, target_owner, target_cell, target_offset):
    slabs_count = NGRID // GS
    channels = panels.shape[0]

    def one_slab(index):
        gpos = index * GS + jnp.arange(GS, dtype=jnp.int32)
        return grid_terms(panels, block_phase, gpos)

    slabs = lax.map(one_slab, jnp.arange(slabs_count, dtype=jnp.int32))
    grid_values = jnp.transpose(slabs, (1, 0, 2)).reshape(channels, NGRID)
    padded = jnp.pad(grid_values, ((0, 0), (TAPS // 2, TAPS // 2)))
    owners = target_owner[:, 0].reshape(slabs_count, TGT_DEV)
    cells = target_cell.reshape(slabs_count, TGT_DEV)
    offsets = target_offset.reshape(slabs_count, TGT_DEV)

    def one_list(items):
        owner_ids, cell_ids, offset_ids = items
        starts = (owner_ids * GS + cell_ids + 1).astype(jnp.int32)
        windows = jax.vmap(lambda begin: lax.dynamic_slice_in_dim(padded, begin, TAPS, 1))(starts)
        kernel = kernel_rows(offset_ids)
        return jnp.einsum("bct,bt->cb", windows, kernel, precision=lax.Precision.HIGHEST)

    values = lax.map(one_list, (owners, cells, offsets))
    target_values = jnp.transpose(values, (1, 0, 2)).reshape(channels, TARGETS)
    return grid_values, target_values
```

```python
import functools
import math

import jax
import jax.numpy as jnp
import ml_dtypes
import numpy as np
from jax import lax
from jax.experimental import pallas as pl
from jax.experimental.pallas import tpu as pltpu
from jax.sharding import PartitionSpec as P

TAPS = 256
OFFQ = 256
GS = 6144
PHASEQ = 4194304
TILE = 512
TILES = GS // TILE
WIN = 256
GROUP = 256
MESH = pl.DeviceIdType.MESH
F32 = jnp.float32
BF16 = jnp.bfloat16


def local_expansion(centers, half, order):
    nodes = np.cos((np.arange(order) + 0.5) * np.pi / order)
    back = np.cos(np.outer(np.arange(order), np.arccos(nodes))) * 2.0 / order
    back[0] *= 0.5
    x = np.asarray(centers, np.float64)[:, None] + half * nodes[None, :]
    tj = np.polynomial.chebyshev.chebvander(x, order - 1)
    return np.einsum("tnj,kn->tjk", tj, back)


def split_np(x):
    hi = x.astype(np.float32).astype(ml_dtypes.bfloat16)
    lo = (x - hi.astype(np.float64)).astype(np.float32).astype(ml_dtypes.bfloat16)
    return hi, lo


def local_cheb(width, order):
    y = (2.0 * np.arange(width) + 1.0) / width - 1.0
    return np.polynomial.chebyshev.chebvander(y, order - 1).T.astype(np.float32)


def tables(order, nblk):
    half = TILE / GS
    centers = (2.0 * TILE * np.arange(TILES) + TILE) / GS - 1.0
    m = local_expansion(centers, half, order)
    eye = np.eye(nblk)
    big = np.einsum("tjk,bc->tjbkc", m, eye).reshape(TILES, order * nblk, order * nblk)
    h = WIN / GS
    nodes = np.cos((np.arange(order) + 0.5) * np.pi / order)
    back = np.cos(np.outer(np.arange(order), np.arccos(nodes))) * 2.0 / order
    back[0] *= 0.5
    a_nodes = local_expansion(nodes * (1.0 - h), h, order)
    series = np.einsum("njk,mn->jkm", a_nodes, back).reshape(order * order, order)
    padded = np.zeros((order * order, 128), np.float64)
    padded[:, :order] = series
    return split_np(big), padded.astype(np.float32)


def split(x):
    hi = x.astype(BF16)
    return hi, (x - hi.astype(F32)).astype(BF16)


def dot3(ah, al, bh, bl):
    out = jnp.dot(ah, bh, preferred_element_type=F32)
    out = out + jnp.dot(al, bh, preferred_element_type=F32)
    return out + jnp.dot(ah, bl, preferred_element_type=F32)


def turned(x):
    half = x.shape[0] // 2
    return jnp.concatenate([-x[half:], x[:half]], 0)


def sincos(turns):
    turns = turns & (PHASEQ - 1)
    quad = (turns + PHASEQ // 8) >> 20
    r = (turns - (quad << 20)).astype(F32) * (2.0 * math.pi / PHASEQ)
    r2 = r * r
    s = r + r * r2 * (-1 / 6 + r2 * (1 / 120 + r2 * (-1 / 5040 + r2 * (1 / 362880))))
    c = 1.0 + r2 * (-0.5 + r2 * (1 / 24 + r2 * (-1 / 720 + r2 * (1 / 40320))))
    odd = (quad & 1) == 1
    sn = jnp.where(odd, c, s)
    cs = jnp.where(odd, s, c)
    sn = jnp.where((quad & 2) == 2, -sn, sn)
    cs = jnp.where(((quad + 1) & 2) == 2, -cs, cs)
    return sn, cs


def gather_kernel(n, pan_ref, ph_ref, pan_out, ph_out, own_sem, send_sem, recv_sem):
    me = lax.axis_index("term")
    barrier = pltpu.get_barrier_semaphore()
    for d in range(1, n):
        pl.semaphore_signal(barrier, inc=1, device_id={"term": lax.rem(me + d, n)}, device_id_type=MESH)
    pl.semaphore_wait(barrier, n - 1)
    pairs = ((pan_ref, pan_out), (ph_ref, ph_out))
    copies = []
    for d in range(1, n):
        for a, (src, dst) in enumerate(pairs):
            copy = pltpu.make_async_remote_copy(
                src_ref=src,
                dst_ref=dst.at[me],
                send_sem=send_sem.at[a, d],
                recv_sem=recv_sem.at[a, d],
                device_id={"term": lax.rem(me + d, n)},
                device_id_type=MESH,
            )
            copy.start()
            copies.append(copy)
    for a, (src, dst) in enumerate(pairs):
        own = pltpu.make_async_copy(src, dst.at[me], own_sem.at[a])
        own.start()
        copies.append(own)
    for copy in copies:
        copy.wait()


def gathered(n, pan, ph):
    return pl.pallas_call(
        functools.partial(gather_kernel, n),
        out_shape=(
            jax.ShapeDtypeStruct((n,) + pan.shape, pan.dtype),
            jax.ShapeDtypeStruct((n,) + ph.shape, ph.dtype),
        ),
        in_specs=[pl.BlockSpec(memory_space=pl.ANY)] * 2,
        out_specs=[pl.BlockSpec(memory_space=pl.ANY)] * 2,
        scratch_shapes=[
            pltpu.SemaphoreType.DMA((2,)),
            pltpu.SemaphoreType.DMA((2, n)),
            pltpu.SemaphoreType.DMA((2, n)),
        ],
        compiler_params=pltpu.CompilerParams(collective_id=0, has_side_effects=True),
    )(pan, ph)


def fill_basis(n, order, nblk, width, ph_ref, cheb_ref, hi_ref, lo_ref):
    lane = lax.broadcasted_iota(jnp.int32, (nblk, width), 1)

    def chunk(i, carry):
        adv = ph_ref[i, 8 : 8 + nblk, 128:129]
        sn, cs = sincos(lane * adv)
        for k in range(order):
            row = cheb_ref[k : k + 1, :]
            for part, wave in enumerate((cs, sn)):
                at = pl.multiple_of((i * 2 + part) * order * nblk + k * nblk, nblk)
                hi, lo = split(wave * row)
                hi_ref[pl.ds(at, nblk), :] = hi
                lo_ref[pl.ds(at, nblk), :] = lo
        return carry

    lax.fori_loop(0, n, chunk, 0)


def grid_kernel(n, order, nblk, pan_ref, ph_ref, cheb_ref, mh_ref, ml_ref, out_ref, bh, bl, ah, al):
    cols = order * nblk
    rows = pan_ref.shape[1]
    device = lax.axis_index("slab") * n + lax.axis_index("term")
    base = device * GS
    fill_basis(n, order, nblk, TILE, ph_ref, cheb_ref, bh, bl)

    def chunk(i, carry):
        ph, pl_ = split(pan_ref[i])
        p0 = ph_ref[i, 0:1, :]
        adv = ph_ref[i, 1:2, :]

        def tile(t, c2):
            z = dot3(ph, pl_, mh_ref[t], ml_ref[t])
            sn, cs = sincos(p0 + (base + t * TILE) * adv)
            q = cs * z + sn * turned(z)
            hi, lo = split(q)
            at = pl.multiple_of(t * rows, rows)
            c0 = pl.multiple_of(i * 2 * cols, 2 * cols)
            ah[pl.ds(at, rows), pl.ds(c0, cols)] = hi
            al[pl.ds(at, rows), pl.ds(c0, cols)] = lo
            c1 = pl.multiple_of(c0 + cols, cols)
            hi2, lo2 = split(turned(q))
            ah[pl.ds(at, rows), pl.ds(c1, cols)] = hi2
            al[pl.ds(at, rows), pl.ds(c1, cols)] = lo2
            return c2

        return lax.fori_loop(0, TILES, tile, carry)

    lax.fori_loop(0, n, chunk, 0)
    mrows = 4 * rows
    for lo_col in range(0, TILE, 256):
        for mb in range(TILES // 4):
            rr = slice(mb * mrows, (mb + 1) * mrows)
            cc = slice(lo_col, lo_col + 256)
            acc = dot3(ah[rr, :], al[rr, :], bh[:, cc], bl[:, cc])
            for t in range(4):
                start = (mb * 4 + t) * TILE + lo_col
                out_ref[:, start : start + 256] = acc[t * rows : (t + 1) * rows]


def target_kernel(
    n, n_dev, order, nblk, pan_ref, ph_ref, cheb_ref, series_ref, own_ref, cell_ref, off_ref, out_ref,
    eh, el, wh, wl, a_ref, u_ref, vh, vl, s_ref,
):
    cols = order * nblk

    @pl.when(pl.program_id(0) == 0)
    def _():
        fill_basis(n, order, nblk, WIN, ph_ref, cheb_ref, eh, el)

    owner = own_ref[...]
    cell = cell_ref[...]
    frac = (off_ref[...].astype(F32) + 0.5) * (1.0 / OFFQ)
    left = cell - (TAPS // 2 - 1) < 0
    right = cell + TAPS // 2 >= GS
    out_ref[...] = jnp.zeros_like(out_ref)

    def piece(slab, start, valid):
        shift = (slab - owner) * GS + start - cell + (TAPS // 2 - 1)
        tap = lax.broadcasted_iota(jnp.int32, (WIN, GROUP), 0)
        place = tap + shift
        inside = (place >= 0) & (place < TAPS) & valid
        dist = (place - TAPS // 2 + 1).astype(F32) - frac
        sgn = jnp.where((place & 1) == 0, 1.0, -1.0)
        sn, _ = sincos((off_ref[...] * 2 + 1) * (PHASEQ // (4 * OFFQ)))
        weights = sgn * sn / (math.pi * dist) * jnp.exp(dist * dist * (-18.0 / (TAPS * TAPS)))
        hi, lo = split(jnp.where(inside, weights, 0.0))
        wh[...] = hi
        wl[...] = lo
        center = (2 * start + WIN - GS).astype(F32) / float(GS - WIN)
        rows = [jnp.ones_like(center), center]
        for j in range(2, order):
            rows.append(2.0 * center * rows[-1] - rows[-2])
        s_ref[...] = jnp.zeros_like(s_ref)
        for j in range(order):
            s_ref[j : j + 1, :] = rows[j]
        a_ref[...] = jnp.dot(
            series_ref[...], s_ref[...], precision=lax.Precision.HIGHEST, preferred_element_type=F32
        )
        first = slab * GS + start

        def chunk(i, carry):
            at = pl.multiple_of(i * 2 * cols, 2 * cols)
            u_ref[...] = dot3(eh[pl.ds(at, 2 * cols), :], el[pl.ds(at, 2 * cols), :], wh[...], wl[...])
            p0 = ph_ref[i, 8 : 8 + nblk, 0:1]
            adv = ph_ref[i, 8 : 8 + nblk, 128:129]
            sn, cs = sincos(p0 + first * adv)
            for b0 in range(0, nblk, 8):
                for l0 in range(0, GROUP, 128):
                    ll = slice(l0, l0 + 128)
                    uc = [u_ref[k * nblk + b0 : k * nblk + b0 + 8, ll] for k in range(order)]
                    us = [u_ref[cols + k * nblk + b0 : cols + k * nblk + b0 + 8, ll] for k in range(order)]
                    s8 = sn[b0 : b0 + 8, ll]
                    c8 = cs[b0 : b0 + 8, ll]
                    for j in range(order):
                        vc = vs = None
                        for k in range(j + 1):
                            a = a_ref[j * order + k : j * order + k + 1, ll]
                            vc = a * uc[k] if vc is None else vc + a * uc[k]
                            vs = a * us[k] if vs is None else vs + a * us[k]
                        u_j = j * nblk + b0
                        s_re = c8 * vc - s8 * vs
                        s_im = s8 * vc + c8 * vs
                        vh[u_j : u_j + 8, ll] = s_re
                        vl[u_j : u_j + 8, ll] = s_im
            ph, pl_ = split(pan_ref[i])
            th, tl = turned(ph), turned(pl_)
            rh, rl = split(vh[...])
            ih, il = split(vl[...])
            out_ref[...] += dot3(ph, pl_, rh, rl) + dot3(th, tl, ih, il)
            return carry

        lax.fori_loop(0, n, chunk, 0)

    start = jnp.clip(cell - (TAPS // 2 - 1), 0, GS - WIN)
    piece(owner, start, jnp.full(cell.shape, True))
    side_ok = (left & (owner > 0)) | (right & (owner < n_dev - 1))

    @pl.when(jnp.max(side_ok.astype(jnp.int32)) > 0)
    def _():
        slab = jnp.where(left, owner - 1, owner + 1)
        piece(slab, jnp.where(left, GS - WIN, 0), side_ok)


def body(n_slab, n, panels, block_phase, target_owner, target_cell, target_offset):
    n_dev = n_slab * n
    channels = panels.shape[0]
    nblk = block_phase.shape[1]
    order = panels.shape[1] // nblk
    cols = order * nblk
    targets = target_cell.shape[0]
    (mh, ml), series = tables(order, nblk)
    pan = panels.reshape(channels, nblk, order).swapaxes(1, 2).reshape(channels, cols)
    wide = jnp.tile(block_phase, (1, order))
    tall = jnp.repeat(block_phase.T, cols // 2, axis=1)
    ph = jnp.concatenate([wide, jnp.zeros((6, cols), jnp.int32), tall], 0)
    pan, ph = gathered(n, pan, ph)
    vmem = pl.BlockSpec(memory_space=pltpu.VMEM)
    grid = pl.pallas_call(
        functools.partial(grid_kernel, n, order, nblk),
        out_shape=jax.ShapeDtypeStruct((channels, GS), F32),
        in_specs=[vmem] * 5,
        out_specs=vmem,
        scratch_shapes=[
            pltpu.VMEM((n * 2 * cols, TILE), BF16),
            pltpu.VMEM((n * 2 * cols, TILE), BF16),
            pltpu.VMEM((TILES * channels, n * 2 * cols), BF16),
            pltpu.VMEM((TILES * channels, n * 2 * cols), BF16),
        ],
        compiler_params=pltpu.CompilerParams(vmem_limit_bytes=48 << 20),
    )(pan, ph, local_cheb(TILE, order), mh, ml)
    lanes = pl.BlockSpec((1, GROUP), lambda g: (0, g))
    values = pl.pallas_call(
        functools.partial(target_kernel, n, n_dev, order, nblk),
        out_shape=jax.ShapeDtypeStruct((channels, targets), F32),
        grid=(targets // GROUP,),
        in_specs=[
            pl.BlockSpec((n, channels, cols), lambda g: (0, 0, 0)),
            pl.BlockSpec(ph.shape, lambda g: (0, 0, 0)),
            pl.BlockSpec((order, WIN), lambda g: (0, 0)),
            pl.BlockSpec(series.shape, lambda g: (0, 0)),
            lanes,
            lanes,
            lanes,
        ],
        out_specs=pl.BlockSpec((channels, GROUP), lambda g: (0, g)),
        scratch_shapes=[
            pltpu.VMEM((n * 2 * cols, WIN), BF16),
            pltpu.VMEM((n * 2 * cols, WIN), BF16),
            pltpu.VMEM((WIN, GROUP), BF16),
            pltpu.VMEM((WIN, GROUP), BF16),
            pltpu.VMEM((order * order, GROUP), F32),
            pltpu.VMEM((2 * cols, GROUP), F32),
            pltpu.VMEM((cols, GROUP), F32),
            pltpu.VMEM((cols, GROUP), F32),
            pltpu.VMEM((128, GROUP), F32),
        ],
        compiler_params=pltpu.CompilerParams(vmem_limit_bytes=48 << 20),
    )(
        pan,
        ph,
        local_cheb(WIN, order),
        series,
        target_owner.reshape(1, targets),
        target_cell.reshape(1, targets),
        target_offset.reshape(1, targets),
    )
    return grid, values


def solution(mesh):
    placed = (
        P(None, "term"),
        P(None, "term"),
        P(("slab", "term"), None),
        P(("slab", "term")),
        P(("slab", "term")),
    )
    return jax.shard_map(
        functools.partial(body, mesh.shape["slab"], mesh.shape["term"]),
        mesh=mesh,
        in_specs=placed,
        out_specs=(P(None, ("slab", "term")), P(None, ("slab", "term"))),
        check_vma=False,
    )
```

```python
import functools
import math

import jax
import jax.numpy as jnp
import ml_dtypes
import numpy as np
from jax import lax
from jax.experimental import pallas as pl
from jax.experimental.pallas import tpu as pltpu
from jax.sharding import PartitionSpec as P

TAPS = 256
OFFQ = 256
GS = 6144
PHASEQ = 4194304
TILE = 1024
TILES = GS // TILE
WIN = 256
GROUP = 256
SIDE = 128
MESH = pl.DeviceIdType.MESH
F32 = jnp.float32
BF16 = jnp.bfloat16


def local_expansion(centers, half, order):
    nodes = np.cos((np.arange(order) + 0.5) * np.pi / order)
    back = np.cos(np.outer(np.arange(order), np.arccos(nodes))) * 2.0 / order
    back[0] *= 0.5
    x = np.asarray(centers, np.float64)[:, None] + half * nodes[None, :]
    tj = np.polynomial.chebyshev.chebvander(x, order - 1)
    return np.einsum("tnj,kn->tjk", tj, back)


def split_np(x):
    hi = x.astype(np.float32).astype(ml_dtypes.bfloat16)
    lo = (x - hi.astype(np.float64)).astype(np.float32).astype(ml_dtypes.bfloat16)
    return hi, lo


def local_cheb(width, order):
    y = (2.0 * np.arange(width) + 1.0) / width - 1.0
    return np.polynomial.chebyshev.chebvander(y, order - 1).T.astype(np.float32)


def tables(order, nblk):
    half = TILE / GS
    centers = (2.0 * TILE * np.arange(TILES) + TILE) / GS - 1.0
    m = local_expansion(centers, half, order)
    eye = np.eye(nblk)
    big = np.einsum("tjk,bc->tbjkc", m, eye).reshape(TILES, order * nblk, order * nblk)
    h = WIN / GS
    nodes = np.cos((np.arange(order) + 0.5) * np.pi / order)
    back = np.cos(np.outer(np.arange(order), np.arccos(nodes))) * 2.0 / order
    back[0] *= 0.5
    a_nodes = local_expansion(nodes * (1.0 - h), h, order)
    series = np.einsum("njk,mn->jkm", a_nodes, back).reshape(order * order, order)
    padded = np.zeros((order * order, 128), np.float64)
    padded[:, :order] = series
    return split_np(big), padded.astype(np.float32)


def split(x):
    hi = x.astype(BF16)
    return hi, (x - hi.astype(F32)).astype(BF16)


def dot3(ah, al, bh, bl):
    out = jnp.dot(ah, bh, preferred_element_type=F32)
    out = out + jnp.dot(al, bh, preferred_element_type=F32)
    return out + jnp.dot(ah, bl, preferred_element_type=F32)


def turned(x):
    half = x.shape[0] // 2
    return jnp.concatenate([-x[half:], x[:half]], 0)


def sincos(turns):
    turns = turns & (PHASEQ - 1)
    quad = (turns + PHASEQ // 8) >> 20
    r = (turns - (quad << 20)).astype(F32) * (2.0 * math.pi / PHASEQ)
    r2 = r * r
    s = r + r * r2 * (-1 / 6 + r2 * (1 / 120 + r2 * (-1 / 5040 + r2 * (1 / 362880))))
    c = 1.0 + r2 * (-0.5 + r2 * (1 / 24 + r2 * (-1 / 720 + r2 * (1 / 40320))))
    odd = (quad & 1) == 1
    sn = jnp.where(odd, c, s)
    cs = jnp.where(odd, s, c)
    sn = jnp.where((quad & 2) == 2, -sn, sn)
    cs = jnp.where(((quad + 1) & 2) == 2, -cs, cs)
    return sn, cs


def gather_kernel(n, pan_ref, ph_ref, pan_out, ph_out, own_sem, send_sem, recv_sem, pass_sem, got_sem):
    me = lax.axis_index("term")
    slab = lax.axis_index("slab")
    core = lax.rem(slab, 2)
    twin = {"slab": slab + 1 - 2 * core}
    half = pan_ref.shape[0] // 2
    mine = pl.ds(pl.multiple_of(core * half, half), half)
    barrier = pltpu.get_barrier_semaphore()
    for d in range(1, n):
        pl.semaphore_signal(barrier, inc=1, device_id={"term": lax.rem(me + d, n)}, device_id_type=MESH)
    pl.semaphore_signal(barrier, inc=1, device_id=twin, device_id_type=MESH)
    pl.semaphore_wait(barrier, n)
    arriving = []
    rest = []
    for d in sorted(range(1, n), key=lambda d: -min(d, n - d)):
        peer = {"term": lax.rem(me + d, n)}
        big = pltpu.make_async_remote_copy(
            src_ref=pan_ref.at[mine],
            dst_ref=pan_out.at[me, mine],
            send_sem=send_sem.at[0, d],
            recv_sem=recv_sem.at[0, d],
            device_id=peer,
            device_id_type=MESH,
        )
        small = pltpu.make_async_remote_copy(
            src_ref=ph_ref,
            dst_ref=ph_out.at[me],
            send_sem=send_sem.at[1, d],
            recv_sem=recv_sem.at[1, d],
            device_id=peer,
            device_id_type=MESH,
        )
        big.start()
        small.start()
        arriving.append((d, big))
        rest.append(small)
    for a, (src, dst) in enumerate(((pan_ref, pan_out), (ph_ref, ph_out))):
        own = pltpu.make_async_copy(src, dst.at[me], own_sem.at[a])
        own.start()
        rest.append(own)
    for d, big in reversed(arriving):
        big.wait_recv()
        origin = lax.rem(me - d + n, n)
        passed = pltpu.make_async_remote_copy(
            src_ref=pan_out.at[origin, mine],
            dst_ref=pan_out.at[origin, mine],
            send_sem=pass_sem.at[d],
            recv_sem=got_sem.at[d],
            device_id=twin,
            device_id_type=MESH,
        )
        passed.start()
        rest.append(passed)
    for _, big in arriving:
        big.wait_send()
    for copy in rest:
        copy.wait()


def gathered(n, pan, ph):
    return pl.pallas_call(
        functools.partial(gather_kernel, n),
        out_shape=(
            jax.ShapeDtypeStruct((n,) + pan.shape, pan.dtype),
            jax.ShapeDtypeStruct((n,) + ph.shape, ph.dtype),
        ),
        in_specs=[pl.BlockSpec(memory_space=pl.ANY)] * 2,
        out_specs=[pl.BlockSpec(memory_space=pl.ANY)] * 2,
        scratch_shapes=[
            pltpu.SemaphoreType.DMA((2,)),
            pltpu.SemaphoreType.DMA((2, n)),
            pltpu.SemaphoreType.DMA((2, n)),
            pltpu.SemaphoreType.DMA((n,)),
            pltpu.SemaphoreType.DMA((n,)),
        ],
        compiler_params=pltpu.CompilerParams(collective_id=0, has_side_effects=True),
    )(pan, ph)


def spread_phases(n, order, nblk, ph_ref, col_ref, row_ref):
    cols = order * nblk
    pick = (
        lax.broadcasted_iota(jnp.int32, (nblk, cols), 1) % nblk
        == lax.broadcasted_iota(jnp.int32, (nblk, cols), 0)
    ).astype(F32)
    eye = pick[:, :nblk]
    for i in range(n):
        values = ph_ref[i].astype(F32)
        row = jnp.dot(values, pick, precision=lax.Precision.HIGHEST, preferred_element_type=F32)
        row_ref[i, 0:2] = row.astype(jnp.int32)
        col = lax.dot_general(
            eye, values, (((1,), (1,)), ((), ())), precision=lax.Precision.HIGHEST, preferred_element_type=F32
        ).astype(jnp.int32)
        col_ref[i, :, 0:128] = jnp.broadcast_to(col[:, 0:1], (nblk, 128))
        col_ref[i, :, 128:256] = jnp.broadcast_to(col[:, 1:2], (nblk, 128))


def fill_basis(n, order, nblk, width, col_ref, cheb_ref, hi_ref, lo_ref):
    lane = lax.broadcasted_iota(jnp.int32, (nblk, width), 1)

    def chunk(i, carry):
        sn, cs = sincos(lane * col_ref[i, :, 128:129])
        for k in range(order):
            row = cheb_ref[k : k + 1, :]
            for part, wave in enumerate((cs, sn)):
                at = pl.multiple_of((i * 2 + part) * order * nblk + k * nblk, nblk)
                hi, lo = split(wave * row)
                hi_ref[pl.ds(at, nblk), :] = hi
                lo_ref[pl.ds(at, nblk), :] = lo
        return carry

    lax.fori_loop(0, n, chunk, 0)


def work_kernel(
    n, n_dev, order, nblk,
    pan_ref, ph_ref, cheb_ref, wcheb_ref, series_ref, own_ref, cell_ref, off_ref, mh_hbm, ml_hbm,
    grid_out, val_ref,
    m_ref, load_sem, store_sem, col_ref, row_ref, bh, bl, ah, al, grid_ref,
    eh, el, wh, wl, a_ref, u_ref, vr, vi, s_ref, pp, acc_ref,
):
    cols = order * nblk
    rows = pan_ref.shape[1]
    count = own_ref.shape[1]
    loads = [pltpu.make_async_copy(src, m_ref.at[a], load_sem.at[a]) for a, src in enumerate((mh_hbm, ml_hbm))]
    for copy in loads:
        copy.start()
    spread_phases(n, order, nblk, ph_ref, col_ref, row_ref)
    fill_basis(n, order, nblk, TILE, col_ref, cheb_ref, bh, bl)
    fill_basis(n, order, nblk, WIN, col_ref, wcheb_ref, eh, el)
    device = lax.axis_index("slab") * n + lax.axis_index("term")
    base = device * GS
    r = lax.broadcasted_iota(jnp.int32, (cols, cols), 0)
    c = lax.broadcasted_iota(jnp.int32, (cols, cols), 1)
    perm = ((r % order == c // nblk) & (r // order == c % nblk)).astype(F32).astype(BF16)
    for copy in loads:
        copy.wait()

    def grid_chunk(i, carry):
        both = jnp.concatenate(split(pan_ref[i]), 0)
        pp[i] = jnp.dot(both, perm, preferred_element_type=F32).astype(BF16)
        p0 = row_ref[i, 0:1, :]
        adv = row_ref[i, 1:2, :]
        c0 = pl.multiple_of(i * 2 * cols, 2 * cols)
        c1 = pl.multiple_of(c0 + cols, cols)
        for t in range(TILES):
            z2 = jnp.dot(both, m_ref[0, t], preferred_element_type=F32)
            z = z2[:rows] + z2[rows:] + jnp.dot(both[:rows], m_ref[1, t], preferred_element_type=F32)
            sn, cs = sincos(p0 + (base + t * TILE) * adv)
            q = cs * z + sn * turned(z)
            hi, lo = split(q)
            rr = slice(t * rows, (t + 1) * rows)
            ah[rr, pl.ds(c0, cols)] = hi
            al[rr, pl.ds(c0, cols)] = lo
            ah[rr, pl.ds(c1, cols)] = turned(hi)
            al[rr, pl.ds(c1, cols)] = turned(lo)
        return carry

    lax.fori_loop(0, n, grid_chunk, 0)
    for lo_col in range(0, TILE, 256):
        cc = slice(lo_col, lo_col + 256)
        acc = dot3(ah[...], al[...], bh[:, cc], bl[:, cc])
        for t in range(TILES):
            start = t * TILE + lo_col
            grid_ref[:, start : start + 256] = acc[t * rows : (t + 1) * rows]
    store = pltpu.make_async_copy(grid_ref, grid_out, store_sem)
    store.start()

    def piece(width, owner, cell, offset, slab, start, valid):
        full = slice(0, width)
        shift = (slab - owner) * GS + start - cell + (TAPS // 2 - 1)
        frac = (offset.astype(F32) + 0.5) * (1.0 / OFFQ)
        place = lax.broadcasted_iota(jnp.int32, (WIN, width), 0) + shift
        inside = (place >= 0) & (place < TAPS) & valid
        dist = (place - TAPS // 2 + 1).astype(F32) - frac
        sgn = jnp.where((place & 1) == 0, 1.0, -1.0)
        sn, _ = sincos((offset * 2 + 1) * (PHASEQ // (4 * OFFQ)))
        weights = sgn * sn / (math.pi * dist) * jnp.exp(dist * dist * (-18.0 / (TAPS * TAPS)))
        hi, lo = split(jnp.where(inside, weights, 0.0))
        wh[:, full] = hi
        wl[:, full] = lo
        center = (2 * start + WIN - GS).astype(F32) / float(GS - WIN)
        tm = [jnp.ones_like(center), center]
        for j in range(2, order):
            tm.append(2.0 * center * tm[-1] - tm[-2])
        s_ref[...] = jnp.zeros_like(s_ref)
        for j in range(order):
            s_ref[j : j + 1, full] = tm[j]
        a_ref[:, full] = jnp.dot(
            series_ref[...], s_ref[:, full], precision=lax.Precision.HIGHEST, preferred_element_type=F32
        )
        first = slab * GS + start
        acc_ref[...] = jnp.zeros_like(acc_ref)

        def chunk(i, carry):
            at = pl.multiple_of(i * 2 * cols, 2 * cols)
            span = pl.ds(at, 2 * cols)
            u_ref[:, full] = dot3(eh[span, :], el[span, :], wh[:, full], wl[:, full])
            sn, cs = sincos(col_ref[i, :, 0:1] + first * col_ref[i, :, 128:129])
            for b0 in range(0, nblk, 8):
                for l0 in range(0, width, 128):
                    ll = slice(l0, l0 + 128)
                    uc = [u_ref[k * nblk + b0 : k * nblk + b0 + 8, ll] for k in range(order)]
                    us = [u_ref[cols + k * nblk + b0 : cols + k * nblk + b0 + 8, ll] for k in range(order)]
                    s8 = sn[b0 : b0 + 8, ll]
                    c8 = cs[b0 : b0 + 8, ll]
                    for j in range(order):
                        vc = vs = None
                        for k in range(j + 1):
                            a = a_ref[j * order + k : j * order + k + 1, ll]
                            vc = a * uc[k] if vc is None else vc + a * uc[k]
                            vs = a * us[k] if vs is None else vs + a * us[k]
                        at_j = j * nblk + b0
                        vr[at_j : at_j + 8, ll] = c8 * vc - s8 * vs
                        vi[at_j : at_j + 8, ll] = s8 * vc + c8 * vs
            both = pp[i]
            ph, pl_ = both[:rows], both[rows:]
            rh, rl = split(vr[:, full])
            ih, il = split(vi[:, full])
            acc_ref[:, full] += dot3(ph, pl_, rh, rl) + dot3(turned(ph), turned(pl_), ih, il)
            return carry

        lax.fori_loop(0, n, chunk, 0)
        return acc_ref[:, full]

    for g in range(0, count, GROUP):
        gg = slice(g, g + GROUP)
        cell = cell_ref[:, gg]
        start = jnp.clip(cell - (TAPS // 2 - 1), 0, GS - WIN)
        val_ref[:, gg] = piece(GROUP, own_ref[:, gg], cell, off_ref[:, gg], own_ref[:, gg], start, cell >= 0)

    owner = own_ref[...]
    cell = cell_ref[...]
    left = cell < TAPS // 2 - 1
    right = cell + TAPS // 2 >= GS
    side = (left & (owner > 0)) | (right & (owner < n_dev - 1))
    sidef = side.astype(F32)
    upto = (
        lax.broadcasted_iota(jnp.int32, (count, count), 0) <= lax.broadcasted_iota(jnp.int32, (count, count), 1)
    ).astype(F32).astype(BF16)
    rank = jnp.dot(sidef.astype(BF16), upto, preferred_element_type=F32).astype(jnp.int32) - 1
    table = jnp.concatenate(
        [owner.astype(F32), cell.astype(F32), off_ref[...].astype(F32), sidef, jnp.zeros((4, count), F32)], 0
    )
    groups = (jnp.sum(side.astype(jnp.int32)) + SIDE - 1) // SIDE

    def side_group(g, carry):
        slot = lax.broadcasted_iota(jnp.int32, (SIDE, count), 0) + g * SIDE
        chosen = ((slot == rank) & side).astype(F32)
        packed = lax.dot_general(
            table, chosen, (((1,), (1,)), ((), ())), precision=lax.Precision.HIGHEST, preferred_element_type=F32
        ).astype(jnp.int32)
        p_owner, p_cell, p_off, p_ok = (packed[a : a + 1] for a in range(4))
        p_left = p_cell < TAPS // 2 - 1
        slab = jnp.where(p_left, p_owner - 1, p_owner + 1)
        out = piece(SIDE, p_owner, p_cell, p_off, slab, jnp.where(p_left, GS - WIN, 0), p_ok > 0)
        hi, lo = split(out)
        put = chosen.astype(BF16)
        val_ref[...] += jnp.dot(hi, put, preferred_element_type=F32) + jnp.dot(lo, put, preferred_element_type=F32)
        return carry

    lax.fori_loop(0, groups, side_group, 0)
    store.wait()


def body(n_slab, n, panels, block_phase, target_owner, target_cell, target_offset):
    n_dev = n_slab * n
    channels = panels.shape[0]
    nblk = block_phase.shape[1]
    order = panels.shape[1] // nblk
    cols = order * nblk
    targets = target_cell.shape[0]
    (mh, ml), series = tables(order, nblk)
    pan, ph = gathered(n, panels, block_phase)
    vmem = pl.BlockSpec(memory_space=pltpu.VMEM)
    hbm = pl.BlockSpec(memory_space=pl.ANY)
    return pl.pallas_call(
        functools.partial(work_kernel, n, n_dev, order, nblk),
        out_shape=(
            jax.ShapeDtypeStruct((channels, GS), F32),
            jax.ShapeDtypeStruct((channels, targets), F32),
        ),
        in_specs=[vmem] * 8 + [hbm] * 2,
        out_specs=(hbm, vmem),
        scratch_shapes=[
            pltpu.VMEM((2, TILES, cols, cols), BF16),
            pltpu.SemaphoreType.DMA((2,)),
            pltpu.SemaphoreType.DMA,
            pltpu.VMEM((n, nblk, 256), jnp.int32),
            pltpu.VMEM((n, 8, cols), jnp.int32),
            pltpu.VMEM((n * 2 * cols, TILE), BF16),
            pltpu.VMEM((n * 2 * cols, TILE), BF16),
            pltpu.VMEM((TILES * channels, n * 2 * cols), BF16),
            pltpu.VMEM((TILES * channels, n * 2 * cols), BF16),
            pltpu.VMEM((channels, GS), F32),
            pltpu.VMEM((n * 2 * cols, WIN), BF16),
            pltpu.VMEM((n * 2 * cols, WIN), BF16),
            pltpu.VMEM((WIN, GROUP), BF16),
            pltpu.VMEM((WIN, GROUP), BF16),
            pltpu.VMEM((order * order, GROUP), F32),
            pltpu.VMEM((2 * cols, GROUP), F32),
            pltpu.VMEM((cols, GROUP), F32),
            pltpu.VMEM((cols, GROUP), F32),
            pltpu.VMEM((128, GROUP), F32),
            pltpu.VMEM((n, 2 * channels, cols), BF16),
            pltpu.VMEM((channels, GROUP), F32),
        ],
        compiler_params=pltpu.CompilerParams(vmem_limit_bytes=56 << 20),
    )(
        pan,
        ph,
        local_cheb(TILE, order),
        local_cheb(WIN, order),
        series,
        target_owner.reshape(1, targets),
        target_cell.reshape(1, targets),
        target_offset.reshape(1, targets),
        mh,
        ml,
    )


def solution(mesh):
    placed = (
        P(None, "term"),
        P(None, "term"),
        P(("slab", "term"), None),
        P(("slab", "term")),
        P(("slab", "term")),
    )
    return jax.shard_map(
        functools.partial(body, mesh.shape["slab"], mesh.shape["term"]),
        mesh=mesh,
        in_specs=placed,
        out_specs=(P(None, ("slab", "term")), P(None, ("slab", "term"))),
        check_vma=False,
    )
```
